32 devices in a mesh: shard: 8 (over z, x), seq: 4 (over y, core).
Axes of the slice: x: 2, y: 2, z: 4, core: 2. Of those that a mesh axis runs over, the one named last changes fastest.
Arguments:
- tokens: bfloat16 [16, 2048, 768], P('shard', 'seq'), may hold values from -6 to 6
- cotangent: bfloat16 [16, 2048, 768], P('shard', 'seq'), may hold values from -6 to 6
- query_weight: bfloat16 [768, 768], P('shard'), may hold values from -0.21875 to 0.21875
- key_weight: bfloat16 [768, 768], P('shard'), may hold values from -0.21875 to 0.21875
- value_weight: bfloat16 [768, 768], P('shard'), may hold values from -0.21875 to 0.21875
- output_weight: bfloat16 [768, 768], P('shard'), may hold values from -0.875 to 0.875
- inner_weight: bfloat16 [768, 3072], P('shard'), may hold values from -0.21875 to 0.21875
- inner_bias: bfloat16 [3072], P('shard'), may hold values from -3 to 3
- outer_weight: bfloat16 [3072, 768], P('shard'), may hold values from -0.109375 to 0.109375
- first_gain: bfloat16 [768], P('shard'), may hold values from 0.25 to 1.75
- first_shift: bfloat16 [768], P('shard'), may hold values from -3 to 3
- second_gain: bfloat16 [768], P('shard'), may hold values from 0.25 to 1.75
- second_shift: bfloat16 [768], P('shard'), may hold values from -3 to 3
- doc_starts: int32 [16, 3], P('shard'), may hold values from 0 to 2047, as said below
- random_blocks: int32 [16, 32, 3], P('shard'), may hold values from 0 to 31
Outputs:
- layer_output: bfloat16 [16, 2048, 768], P('shard', 'seq')
- input_grad: bfloat16 [16, 2048, 768], P('shard', 'seq')
- query_grad: float32 [768, 768], P('shard')
- key_grad: float32 [768, 768], P('shard')
- value_grad: float32 [768, 768], P('shard')
- projection_grad: float32 [768, 768], P('shard')
- inner_grad: float32 [768, 3072], P('shard')
- inner_bias_grad: float32 [3072], P('shard')
- outer_grad: float32 [3072, 768], P('shard')
- first_gain_grad: float32 [768], P('shard')
- first_shift_grad: float32 [768], P('shard')
- second_gain_grad: float32 [768], P('shard')
- second_shift_grad: float32 [768], P('shard')
The draws below stay inside these ranges and needn't reach their ends.
Inputs may be any that keep to these rules, and one draw needn't show every extreme that they name: `doc_starts`: each sequence has 3 distinct starts in increasing order, the first 0, all below 2048; the last start of the first sequence is 2047.
All inputs are finite; a program needn't handle non-finite values.
Results may differ from the reference program's by a relative error of at most 0.017.
Values may be sent and summed in bfloat16 or wider, within the bound.
No kernel may reach another device: no remote copies, remote signals or barrier semaphores. Data moves between devices by JAX's collectives and lax.ppermute only.
A program may use at most 320 MiB of HBM per device.

```python
import math
import jax
import jax.numpy as jnp
from jax import lax

H = 12
HD = 64
D = 768
FF = 3072
SEQ = 2048
BLK = 64
NRAND = 3
NDOC = 3
NB = 32
ROWS = 16


def draw_doc_starts(key, part):
    row_keys = jax.random.split(key, ROWS)
    row_numbers = jnp.arange(ROWS, dtype=jnp.int32)

    def one_row(row_key, row_number):
        shuffled = jax.random.permutation(row_key, SEQ - 2) + 1
        chosen = jnp.sort(shuffled[:NDOC - 1]).astype(jnp.int32)
        final = jnp.where(row_number == 0, jnp.int32(SEQ - 1), chosen[NDOC - 2])
        chosen = chosen.at[NDOC - 2].set(final)
        return jnp.concatenate([jnp.zeros((1,), jnp.int32), chosen])
    return jax.vmap(one_row)(row_keys, row_numbers)


def place_ends(values, stream_key, least, high):
    index_at = [jax.random.randint(jax.random.fold_in(stream_key, axis), (), 0, length) for axis, length in enumerate(values.shape)]
    longest = values.shape.index(max(values.shape))
    beside = index_at[:longest] + [(index_at[longest] + 1) % values.shape[longest]] + index_at[longest + 1:]
    return values.at[tuple(index_at)].set(least).at[tuple(beside)].set(high)


def spiked(values, rng, source, target, blocks, factor):
    owner, partner = [(jnp.arange(values.shape[dim]) // (values.shape[dim] // blocks)).reshape([-1 if axis == dim else 1 for axis in range(values.ndim)]) for dim in (source, target)]
    chosen = jax.random.permutation(rng, blocks)[partner]
    strong = (owner == chosen) | (owner == (partner + blocks // 2) % blocks)
    return jnp.where(strong, factor * values, values)


def levels(rng, extent, cuts, least, largest):
    level = 1.0
    for axis_at, blocks in cuts:
        draws = jax.random.uniform(jax.random.fold_in(jax.random.fold_in(rng, 6), axis_at), (blocks,), jnp.float32, least / len(cuts), largest / len(cuts))
        level = level * jnp.repeat(jnp.exp(draws), extent[axis_at] // blocks).reshape((-1,) + (1,) * (len(extent) - 1 - axis_at))
    return level


def normal_values(own_key, shape, scale, reach, cuts=(), kind=jnp.bfloat16):
    values = scale * jax.random.normal(own_key, shape, jnp.float32)
    if cuts:
        values = values * levels(own_key, shape, cuts, -0.22, 0.18)
    return jnp.clip(values, -reach, reach).astype(kind)


def noise_with(stream_key, dims, scale, bound, shards, heavy, kind=jnp.bfloat16):
    drawn = scale * jax.random.normal(stream_key, dims, jnp.float32)
    if shards:
        drawn = drawn * levels(stream_key, dims, shards, -0.22, 0.18)
    return jnp.clip(spiked(drawn, jax.random.fold_in(stream_key, 3), *heavy), -bound, bound).astype(kind)


def setup_inputs(seed: int = 0) -> dict:
    key_list = jax.random.split(jax.random.key(seed), 16)
    tokens = normal_values(key_list[0], (ROWS, SEQ, D), 1.0, 6.0, ((0, 8), (1, 4)))
    cotangent = noise_with(key_list[1], (ROWS, SEQ, D), 1.0, 6.0, ((0, 8), (1, 4)), (0, 2, 8, 2.0))
    query_weight = normal_values(key_list[2], (D, D), D ** -0.5, 0.21875, ((0, 8),))
    key_weight = normal_values(key_list[3], (D, D), D ** -0.5, 0.21875, ((0, 8),))
    value_weight = normal_values(key_list[4], (D, D), D ** -0.5, 0.21875, ((0, 8),))
    output_weight = normal_values(key_list[5], (D, D), (D // 16) ** -0.5, 0.875, ((0, 8),))
    inner_weight = normal_values(key_list[6], (D, FF), D ** -0.5, 0.21875, ((0, 8),))
    inner_bias = normal_values(key_list[7], (FF,), 0.5, 3.0, ((0, 8),))
    outer_weight = normal_values(key_list[8], (FF, D), FF ** -0.5, 0.109375, ((0, 8),))
    first_gain = jnp.clip(1.0 + 0.15 * jax.random.normal(key_list[9], (D,), jnp.float32), 0.25, 1.75).astype(jnp.bfloat16)
    first_shift = normal_values(key_list[10], (D,), 0.5, 3.0, ((0, 8),))
    second_gain = jnp.clip(1.0 + 0.15 * jax.random.normal(key_list[11], (D,), jnp.float32), 0.25, 1.75).astype(jnp.bfloat16)
    second_shift = normal_values(key_list[12], (D,), 0.5, 3.0, ((0, 8),))
    doc_starts = draw_doc_starts(jax.random.fold_in(key_list[15], 71), 0)
    random_blocks = place_ends(jax.random.randint(key_list[14], (ROWS, NB, NRAND), 0, NB), jax.random.fold_in(key_list[14], 1), 0, NB - 1).astype(jnp.int32)
    return {"tokens": tokens, "cotangent": cotangent, "query_weight": query_weight, "key_weight": key_weight, "value_weight": value_weight, "output_weight": output_weight, "inner_weight": inner_weight, "inner_bias": inner_bias, "outer_weight": outer_weight, "first_gain": first_gain, "first_shift": first_shift, "second_gain": second_gain, "second_shift": second_shift, "doc_starts": doc_starts, "random_blocks": random_blocks}


@jax.custom_vjp
def low(v):
    return lax.optimization_barrier(v.astype(jnp.bfloat16)).astype(jnp.float32)

@jax.custom_vjp
def low_back(v):
    return v

def low_keep(v):
    return (low(v), None)

def low_pass(kept, grad):
    return (grad,)

def back_keep(v):
    return (v, None)

def back_low(kept, grad):
    return (low(grad),)
low.defvjp(low_keep, low_pass)
low_back.defvjp(back_keep, back_low)
EPS = 1e-06

def layer_norm(values, gain, shift):
    centered = values - lax.optimization_barrier(jnp.mean(values, axis=-1, keepdims=True))
    spread = lax.optimization_barrier(jnp.mean(centered * centered, axis=-1, keepdims=True))
    return centered * lax.rsqrt(spread + EPS) * gain + shift

def activate(values):
    return jax.nn.gelu(values, approximate=True)

def block_mask(starts, chosen, seq_len, width):
    blocks = seq_len // width
    places = jnp.arange(seq_len, dtype=jnp.int32)
    segment = lax.optimization_barrier(jnp.sum((starts[None, :] <= places[:, None]).astype(jnp.int32), axis=1))
    follow = jnp.concatenate([starts[1:], jnp.full((1,), seq_len, jnp.int32)])
    first_block = starts // width
    last_block = (follow - 1) // width
    numbers = jnp.arange(blocks, dtype=jnp.int32)
    special = jnp.any(first_block[None, :] == numbers[:, None], axis=1) | jnp.any(last_block[None, :] == numbers[:, None], axis=1)
    nearby = jnp.abs(numbers[:, None] - numbers[None, :]) <= 1
    picked = jnp.any(chosen[:, :, None] == numbers[None, None, :], axis=1)
    blocked = nearby | special[:, None] | special[None, :] | picked
    expanded = jnp.repeat(jnp.repeat(blocked, width, axis=0), width, axis=1)
    return expanded & (segment[:, None] == segment[None, :])

def forward(row, query_weight, key_weight, value_weight, output_weight, inner_weight, inner_bias, outer_weight, first_gain, first_shift, second_gain, second_shift, attend):
    highest = lax.Precision.HIGHEST
    queries = low(low_back(jnp.dot(row, query_weight, precision=highest))).reshape(SEQ, H, HD)
    keys_all = low(low_back(jnp.dot(row, key_weight, precision=highest))).reshape(SEQ, H, HD)
    values_all = low(low_back(jnp.dot(row, value_weight, precision=highest))).reshape(SEQ, H, HD)
    scores_raw = jnp.einsum('qhd,khd->hqk', queries, keys_all, precision=highest)
    scores = low_back(scores_raw) * (1.0 / math.sqrt(HD))
    scores = jnp.where(attend[None], scores, -1000000000.0)
    highest_score = lax.optimization_barrier(jnp.max(scores, axis=-1, keepdims=True))
    expd = jnp.exp(scores - highest_score)
    probs = expd / lax.optimization_barrier(jnp.sum(expd, axis=-1, keepdims=True))
    context = jnp.einsum('hqk,khd->qhd', low(probs), values_all, precision=highest).reshape(SEQ, H * HD)
    context = low(low_back(context))
    attended = low_back(jnp.dot(context, output_weight, precision=highest))
    first = layer_norm(row + attended, first_gain, first_shift)
    inner = low_back(jnp.dot(low(first), inner_weight, precision=highest) + inner_bias)
    outer = low_back(jnp.dot(low(activate(inner)), outer_weight, precision=highest))
    return layer_norm(first + outer, second_gain, second_shift)

def reference(tokens, cotangent, query_weight, key_weight, value_weight, output_weight, inner_weight, inner_bias, outer_weight, first_gain, first_shift, second_gain, second_shift, doc_starts, random_blocks):
    params = tuple((item.astype(jnp.float32) for item in (query_weight, key_weight, value_weight, output_weight, inner_weight, inner_bias, outer_weight, first_gain, first_shift, second_gain, second_shift)))

    def one_row(totals, inputs):
        row, grad_row, starts, chosen = inputs
        attend = block_mask(starts, chosen, SEQ, BLK)

        def run(row_in, *weights):
            return forward(row_in, *weights, attend)
        result, pull = jax.vjp(run, row, *params)
        grads = pull(grad_row)
        updated = tuple((old + new for old, new in zip(totals, grads[1:])))
        return (updated, (result.astype(jnp.bfloat16), grads[0].astype(jnp.bfloat16)))
    zeros = tuple((jnp.zeros(item.shape, jnp.float32) for item in params))
    totals, (outputs, input_grads) = lax.scan(one_row, zeros, (tokens.astype(jnp.float32), cotangent.astype(jnp.float32), doc_starts, random_blocks))
    return (outputs, input_grads, totals[0], totals[1], totals[2], totals[3], totals[4], totals[5], totals[6], totals[7], totals[8], totals[9], totals[10])
```

```python
import jax
import jax.numpy as jnp
from jax import lax
from jax.experimental import pallas as pl
from jax.experimental.pallas import tpu as pltpu
from jax.sharding import PartitionSpec as P

H = 12
HD = 64
EPS = 1e-06
BLK=64; PAIR=128; GRP=4
F32=jnp.float32; BF=jnp.bfloat16

def nt(a,b): return lax.dot_general(a,b,(((1,),(1,)),((),())),preferred_element_type=F32)
def tn(a,b): return lax.dot_general(a,b,(((0,),(0,)),((),())),preferred_element_type=F32)
def nn(a,b): return lax.dot_general(a,b,(((1,),(0,)),((),())),preferred_element_type=F32)

def fwd_call(mine, recv, qmask, kmask, idx, cnt):
    half=mine.shape[0]; seq=2*half; nb=seq//BLK; width=mine.shape[1]//3; pairs=width//PAIR
    rows=2*BLK; gk=GRP*BLK; maxg=nb//GRP
    def kern(idx_ref,cnt_ref,mine_ref,recv_ref,qm_ref,km_ref,out_ref,log_ref,kx,vx,s_scr,mx,acc,ls):
        lane=lax.broadcasted_iota(jnp.int32,(BLK,PAIR),1)
        low=lane<BLK
        for p in range(pairs):
            for t,src in ((0,mine_ref),(1,recv_ref)):
                kx[p,t*half:(t+1)*half,:PAIR]=src[:,width+p*PAIR:width+(p+1)*PAIR]
                vx[p,t*half:(t+1)*half,:]=src[:,2*width+p*PAIR:2*width+(p+1)*PAIR]
            kx[p,seq:seq+BLK,:PAIR]=jnp.zeros((BLK,PAIR),BF)
            vx[p,seq:seq+BLK,:]=jnp.zeros((BLK,PAIR),BF)
            kx[p,:,PAIR:]=km_ref[...]
        def half_loop(src_ref,base):
            def qblock(b,_):
                i=base+b
                n=cnt_ref[i]
                qrow=pl.multiple_of(b*BLK,BLK)
                qm=qm_ref[pl.ds(pl.multiple_of(i*BLK,BLK),BLK),:]
                qs=[]
                for p in range(pairs):
                    q=src_ref[pl.ds(qrow,BLK),p*PAIR:(p+1)*PAIR]*jnp.asarray(0.125,BF)
                    z=jnp.zeros_like(q)
                    stk=jnp.concatenate([jnp.where(low,q,z),jnp.where(low,z,q)],axis=0)
                    qs.append(jnp.concatenate([stk,jnp.concatenate([qm,qm],axis=0)],axis=1))
                    mx[p]=jnp.full((rows,PAIR),-3e38,F32)
                    ls[p]=jnp.zeros((rows,PAIR),F32)
                    acc[p]=jnp.zeros((rows,PAIR),F32)
                def p1(g,_):
                    at=[pl.multiple_of(idx_ref[i,g*GRP+j]*BLK,BLK) for j in range(GRP)]
                    for p in range(pairs):
                        kg=jnp.concatenate([kx[p,pl.ds(a,BLK),:] for a in at],axis=0)
                        s=nt(qs[p],kg)
                        s_scr[g,p]=s
                        mx[p]=jnp.maximum(mx[p],jnp.maximum(s[:,:PAIR],s[:,PAIR:]))
                    return 0
                lax.fori_loop(0,n,p1,0)
                ms=[jnp.max(mx[p],axis=1,keepdims=True) for p in range(pairs)]
                def p2(g,_):
                    at=[pl.multiple_of(idx_ref[i,g*GRP+j]*BLK,BLK) for j in range(GRP)]
                    for p in range(pairs):
                        vg=jnp.concatenate([vx[p,pl.ds(a,BLK),:] for a in at],axis=0)
                        e=jnp.exp(s_scr[g,p]-ms[p])
                        ls[p]=ls[p]+(e[:,:PAIR]+e[:,PAIR:])
                        acc[p]=acc[p]+nn(e.astype(BF),vg)
                    return 0
                lax.fori_loop(0,n,p2,0)
                lanes=lax.broadcasted_iota(jnp.int32,(rows,PAIR),1)
                logs=jnp.zeros((rows,PAIR),F32)
                for p in range(pairs):
                    l=jnp.sum(ls[p],axis=1,keepdims=True)
                    o=acc[p]*(1.0/l)
                    o=jnp.where(low,o[:BLK],o[BLK:])
                    out_ref[pl.ds(pl.multiple_of(i*BLK,BLK),BLK),p*PAIR:(p+1)*PAIR]=o.astype(BF)
                    logs=jnp.where(lanes==p,ms[p]+jnp.log(l),logs)
                log_ref[pl.ds(pl.multiple_of(i*rows,rows),rows),:]=logs
                return 0
            lax.fori_loop(0,nb//2,qblock,0)
        half_loop(mine_ref,0)
        half_loop(recv_ref,nb//2)
    v=pl.BlockSpec(memory_space=pltpu.VMEM)
    s=pl.BlockSpec(memory_space=pltpu.SMEM)
    return pl.pallas_call(kern,name="attn_fwd",
        out_shape=(jax.ShapeDtypeStruct((seq,width),BF),jax.ShapeDtypeStruct((nb*rows,PAIR),F32)),
        in_specs=[s,s,v,v,v,v],out_specs=(v,v),
        scratch_shapes=[pltpu.VMEM((pairs,seq+BLK,2*PAIR),BF),pltpu.VMEM((pairs,seq+BLK,PAIR),BF),
            pltpu.VMEM((maxg,pairs,rows,gk),F32),pltpu.VMEM((pairs,rows,PAIR),F32),pltpu.VMEM((pairs,rows,PAIR),F32),pltpu.VMEM((pairs,rows,PAIR),F32)],
        cost_estimate=pl.CostEstimate(flops=20_000_000_000,transcendentals=12_000_000,bytes_accessed=12_000_000),
    )(idx,cnt,mine,recv,qmask,kmask)

def bwd_call(mine, recv, dmine, drecv, out, logs, qmask, kmask, idx, cnt):
    half=mine.shape[0]; seq=2*half; nb=seq//BLK; width=mine.shape[1]//3; pairs=width//PAIR
    rows=2*BLK; gk=GRP*BLK
    def kern(idx_ref,cnt_ref,mine_ref,recv_ref,dm_ref,dr_ref,o_ref,log_ref,qm_ref,km_ref,g_ref,kx,vx,dk,dv,dq):
        lane=lax.broadcasted_iota(jnp.int32,(BLK,PAIR),1)
        low=lane<BLK
        for p in range(pairs):
            for t,src in ((0,mine_ref),(1,recv_ref)):
                kx[p,t*half:(t+1)*half,:PAIR]=src[:,width+p*PAIR:width+(p+1)*PAIR]
                vx[p,t*half:(t+1)*half,:]=src[:,2*width+p*PAIR:2*width+(p+1)*PAIR]
            kx[p,seq:seq+BLK,:PAIR]=jnp.zeros((BLK,PAIR),BF)
            vx[p,seq:seq+BLK,:]=jnp.zeros((BLK,PAIR),BF)
            kx[p,:,PAIR:]=km_ref[...]
            dk[p]=jnp.zeros((seq+BLK,PAIR),F32)
            dv[p]=jnp.zeros((seq+BLK,PAIR),F32)
        def half_loop(src_ref,dsrc_ref,base):
            def qblock(b,_):
                i=base+b
                n=cnt_ref[i]
                qrow=pl.multiple_of(b*BLK,BLK)
                irow=pl.multiple_of(i*BLK,BLK)
                qm=qm_ref[pl.ds(irow,BLK),:]
                logs=log_ref[pl.ds(pl.multiple_of(i*rows,rows),rows),:]
                qs=[];ds_=[];ls_=[];dl=[]
                for p in range(pairs):
                    q=src_ref[pl.ds(qrow,BLK),p*PAIR:(p+1)*PAIR]*jnp.asarray(0.125,BF)
                    z=jnp.zeros_like(q)
                    stk=jnp.concatenate([jnp.where(low,q,z),jnp.where(low,z,q)],axis=0)
                    qs.append(jnp.concatenate([stk,jnp.concatenate([qm,qm],axis=0)],axis=1))
                    d=dsrc_ref[pl.ds(qrow,BLK),p*PAIR:(p+1)*PAIR]
                    ds_.append(jnp.concatenate([jnp.where(low,d,z),jnp.where(low,z,d)],axis=0))
                    prod=d.astype(F32)*o_ref[pl.ds(irow,BLK),p*PAIR:(p+1)*PAIR].astype(F32)
                    zf=jnp.zeros_like(prod)
                    dl.append(jnp.sum(jnp.concatenate([jnp.where(low,prod,zf),jnp.where(low,zf,prod)],axis=0),axis=1,keepdims=True))
                    ls_.append(logs[:,p:p+1])
                    dq[p]=jnp.zeros((rows,PAIR),F32)
                def step(g,_):
                    at=[pl.multiple_of(idx_ref[i,g*GRP+j]*BLK,BLK) for j in range(GRP)]
                    for p in range(pairs):
                        kg=jnp.concatenate([kx[p,pl.ds(a,BLK),:] for a in at],axis=0)
                        vg=jnp.concatenate([vx[p,pl.ds(a,BLK),:] for a in at],axis=0)
                        s=nt(qs[p],kg)
                        e=jnp.exp(s-ls_[p])
                        dp=nt(ds_[p],vg)
                        dsc=(e*(dp-dl[p])).astype(BF)
                        dq[p]=dq[p]+nn(dsc,kg[:,:PAIR])
                        dkg=tn(dsc,qs[p][:,:PAIR])
                        dvg=tn(e.astype(BF),ds_[p])
                        for j,a in enumerate(at):
                            dk[p,pl.ds(a,BLK),:]=dk[p,pl.ds(a,BLK),:]+dkg[j*BLK:(j+1)*BLK]
                            dv[p,pl.ds(a,BLK),:]=dv[p,pl.ds(a,BLK),:]+dvg[j*BLK:(j+1)*BLK]
                    return 0
                lax.fori_loop(0,n,step,0)
                for p in range(pairs):
                    g=dq[p]
                    g_ref[pl.ds(irow,BLK),p*PAIR:(p+1)*PAIR]=(jnp.where(low,g[:BLK],g[BLK:])*0.125).astype(BF)
                return 0
            lax.fori_loop(0,nb//2,qblock,0)
        half_loop(mine_ref,dm_ref,0)
        half_loop(recv_ref,dr_ref,nb//2)
        for p in range(pairs):
            g_ref[:,width+p*PAIR:width+(p+1)*PAIR]=dk[p,:seq].astype(BF)
            g_ref[:,2*width+p*PAIR:2*width+(p+1)*PAIR]=dv[p,:seq].astype(BF)
    v=pl.BlockSpec(memory_space=pltpu.VMEM)
    s=pl.BlockSpec(memory_space=pltpu.SMEM)
    return pl.pallas_call(kern,name="attn_bwd",
        out_shape=jax.ShapeDtypeStruct((seq,3*width),BF),
        in_specs=[s,s,v,v,v,v,v,v,v,v],out_specs=v,
        scratch_shapes=[pltpu.VMEM((pairs,seq+BLK,2*PAIR),BF),pltpu.VMEM((pairs,seq+BLK,PAIR),BF),
            pltpu.VMEM((pairs,seq+BLK,PAIR),F32),pltpu.VMEM((pairs,seq+BLK,PAIR),F32),pltpu.VMEM((pairs,rows,PAIR),F32)],
        cost_estimate=pl.CostEstimate(flops=50_000_000_000,transcendentals=12_000_000,bytes_accessed=18_000_000),
    )(idx,cnt,mine,recv,dmine,drecv,out,logs,qmask,kmask)

def tables(starts, chosen, orig, seq):
    nb=orig.shape[0]
    follow=jnp.concatenate([starts[1:],jnp.full((1,),seq,jnp.int32)])-1
    fb=starts//BLK; lb=follow//BLK
    special=jnp.any(fb[None,:]==orig[:,None],axis=1)|jnp.any(lb[None,:]==orig[:,None],axis=1)
    nearby=jnp.abs(orig[:,None]-orig[None,:])<=1
    picked=jnp.any(chosen[:,:,None]==orig[None,None,:],axis=1)
    allowed=nearby|special[:,None]|special[None,:]|picked
    lo=jnp.sum((starts[None,:]<=(orig*BLK)[:,None]).astype(jnp.int32),axis=1)
    hi=jnp.sum((starts[None,:]<=(orig*BLK+BLK-1)[:,None]).astype(jnp.int32),axis=1)
    allowed=allowed&(lo[:,None]<=hi[None,:])&(lo[None,:]<=hi[:,None])
    a=allowed.astype(jnp.int32)
    before=jnp.arange(nb)
    rank=jnp.sum(jnp.where((before[None,:]<before[:,None])[None],a[:,None,:],0),axis=2)
    hit=(rank[:,:,None]==before[None,None,:])&allowed[:,:,None]
    idx=nb+jnp.sum(jnp.where(hit,before[None,:,None]-nb,0),axis=1)
    cnt=(jnp.sum(a,axis=1)+GRP-1)//GRP
    pos=(orig[:,None]*BLK+jnp.arange(BLK)[None,:]).reshape(-1)
    seg=jnp.sum((starts[None,:]<=pos[:,None]).astype(jnp.int32),axis=1)-1
    col=jnp.arange(PAIR)[None,:]
    nd=starts.shape[0]
    qmask=jnp.where((col<=nd)&(col!=seg[:,None]),-1e9,0.0).astype(BF)
    kseg=jnp.concatenate([seg,jnp.full((BLK,),nd,jnp.int32)])
    kmask=(col==kseg[:,None]).astype(BF)
    return idx.astype(jnp.int32),cnt.astype(jnp.int32),qmask,kmask


def swap(value, flip, groups):
    return lax.ppermute(value, "seq", [(s, s ^ flip) for s in range(groups)])


def halves(full, c, width):
    parts = full.reshape(full.shape[0], -1, 2, width)
    own = lax.dynamic_index_in_dim(parts, c, 2, keepdims=False)
    other = lax.dynamic_index_in_dim(parts, 1 - c, 2, keepdims=False)
    return own.reshape(full.shape[0], -1), other.reshape(full.shape[0], -1)


def join(own, other, c, width):
    a = own.reshape(own.shape[0], -1, 1, width)
    b = other.reshape(other.shape[0], -1, 1, width)
    both = jnp.where(c == 0, jnp.concatenate([a, b], 2), jnp.concatenate([b, a], 2))
    return both.reshape(own.shape[0], -1)


def gather_rows(local, s, groups):
    part = local.shape[0] // groups
    mine = lax.dynamic_slice_in_dim(local, s * part, part, 0)
    return lax.all_gather(mine, ("shard", "seq"), axis=0, tiled=True)


def scatter_rows(grad):
    share = lax.psum_scatter(grad.astype(BF), ("shard", "seq"), scatter_dimension=0, tiled=True)
    return lax.all_gather(share, "seq", axis=0, tiled=True).astype(F32)


def body(tokens, cotangent, query_weight, key_weight, value_weight, output_weight, inner_weight,
         inner_bias, outer_weight, first_gain, first_shift, second_gain, second_shift, doc_starts, random_blocks):
    groups = lax.axis_size("seq")
    shards = lax.axis_size("shard")
    rows, local, width = tokens.shape
    assert rows == 2 and groups == 4
    seq = local * groups
    s = lax.axis_index("seq")
    c = s % 2
    y = s // 2
    flip = 2
    hw = (H // 2) * HD

    def bring(pair):
        own = lax.dynamic_index_in_dim(pair, y, 0, keepdims=False)
        away = swap(lax.dynamic_index_in_dim(pair, 1 - y, 0, keepdims=False), flip, groups)
        return jnp.concatenate([own, away], axis=0)

    def give_back(value):
        own = value[:local]
        away = swap(value[local:], flip, groups)
        return jnp.where(y == 0, jnp.stack([own, away]), jnp.stack([away, own]))

    x = bring(tokens)
    cot = bring(cotangent).astype(F32)
    joined_local = jnp.concatenate([query_weight, key_weight, value_weight], axis=1)
    joined = gather_rows(joined_local, s, groups)
    small_local = jnp.concatenate([inner_bias, first_gain, first_shift, second_gain, second_shift])
    small = lax.all_gather(small_local, "shard", axis=0, tiled=False).astype(F32)
    output_full = gather_rows(output_weight, s, groups)
    inner_full = gather_rows(inner_weight, s, groups)
    outer_full = gather_rows(outer_weight, s, groups)
    cuts = [0]
    for item in (inner_bias, first_gain, first_shift, second_gain, second_shift):
        cuts.append(cuts[-1] + item.shape[0])
    bias, gain_one, shift_one, gain_two, shift_two = [
        small[:, a:b].reshape(-1) for a, b in zip(cuts[:-1], cuts[1:])
    ]

    nb = seq // BLK
    per = nb // groups
    quarters = jnp.stack([s, s ^ 2, s ^ 1, s ^ 3])
    orig = (quarters[:, None] * per + jnp.arange(per)[None, :]).reshape(-1).astype(jnp.int32)
    starts = lax.dynamic_index_in_dim(doc_starts, y, 0, keepdims=False)
    chosen = lax.dynamic_index_in_dim(random_blocks, y, 0, keepdims=False)
    chosen = jnp.sum(jnp.where((orig[:, None] == jnp.arange(nb)[None, :])[:, :, None], chosen[None], 0), axis=1)
    idx, cnt, qmask, kmask = tables(starts, chosen, orig, seq)

    w_own, w_sib = halves(joined, c, hw)
    sib_qkv = nn(x, w_sib).astype(BF)
    recv_qkv = swap(sib_qkv, 1, groups)
    own_qkv = nn(x, w_own).astype(BF)
    context_all, logs = fwd_call(own_qkv, recv_qkv, qmask, kmask, idx, cnt)
    ctx_own = context_all[: 2 * local]
    ctx_sib = swap(context_all[2 * local :], 1, groups)
    context = join(ctx_own, ctx_sib, c, hw)
    attended = nn(context, output_full)
    res_one = x.astype(F32) + attended
    cen = res_one - jnp.mean(res_one, axis=-1, keepdims=True)
    rstd_one = lax.rsqrt(jnp.mean(cen * cen, axis=-1, keepdims=True) + EPS)
    n_one = cen * rstd_one
    first = n_one * gain_one + shift_one
    first_low = first.astype(BF)
    inner = nn(first_low, inner_full) + bias
    root = 0.7978845608028654
    tanh = jnp.tanh(root * (inner + 0.044715 * inner * inner * inner))
    active = (0.5 * inner * (1.0 + tanh)).astype(BF)
    slope = 0.5 * (1.0 + tanh) + 0.5 * inner * (1.0 - tanh * tanh) * root * (1.0 + 3 * 0.044715 * inner * inner)
    outer = nn(active, outer_full)
    res_two = first + outer
    cen2 = res_two - jnp.mean(res_two, axis=-1, keepdims=True)
    rstd_two = lax.rsqrt(jnp.mean(cen2 * cen2, axis=-1, keepdims=True) + EPS)
    n_two = cen2 * rstd_two
    result = give_back((n_two * gain_two + shift_two).astype(BF))
    g_two = cot * gain_two
    d_second = (g_two - jnp.mean(g_two, -1, keepdims=True) - n_two * jnp.mean(g_two * n_two, -1, keepdims=True)) * rstd_two
    d_gain_two = jnp.sum(cot * n_two, axis=0)
    d_shift_two = jnp.sum(cot, axis=0)
    d_outer = d_second.astype(BF)
    outer_grad = scatter_rows(tn(active, d_outer))
    d_inner = (nt(d_outer, outer_full) * slope).astype(BF)
    d_bias = jnp.sum(d_inner.astype(F32), axis=0)
    inner_grad = scatter_rows(tn(first_low, d_inner))
    d_first = d_second + nt(d_inner, inner_full)
    d_gain_one = jnp.sum(d_first * n_one, axis=0)
    d_shift_one = jnp.sum(d_first, axis=0)
    k_one = d_first * gain_one
    d_res = (k_one - jnp.mean(k_one, -1, keepdims=True) - n_one * jnp.mean(k_one * n_one, -1, keepdims=True)) * rstd_one
    d_attended = d_res.astype(BF)
    projection_grad = scatter_rows(tn(context, d_attended))
    d_context = nt(d_attended, output_full).astype(BF)
    dc_own, dc_sib = halves(d_context, c, hw)
    dc_recv = swap(dc_sib, 1, groups)
    d_qkv = bwd_call(own_qkv, recv_qkv, dc_own, dc_recv, context_all, logs, qmask, kmask, idx, cnt)
    d_own = d_qkv[: 2 * local]
    d_sib = swap(d_qkv[2 * local :], 1, groups)
    d_input = d_res + nt(d_own, w_own) + nt(d_sib, w_sib)
    input_grad = give_back(d_input.astype(BF))
    joined_grad = scatter_rows(join(tn(x, d_own), tn(x, d_sib), c, hw))
    vec = [v.reshape(shards, -1) for v in (d_bias, d_gain_one, d_shift_one, d_gain_two, d_shift_two)]
    vec = lax.psum(lax.psum_scatter(jnp.concatenate(vec, axis=1), "shard", scatter_dimension=0, tiled=True), "seq")[0]
    vecs = [vec[a:b] for a, b in zip(cuts[:-1], cuts[1:])]
    return (
        result,
        input_grad,
        joined_grad[:, :width],
        joined_grad[:, width : 2 * width],
        joined_grad[:, 2 * width :],
        projection_grad,
        inner_grad,
        vecs[0],
        outer_grad,
        vecs[1],
        vecs[2],
        vecs[3],
        vecs[4],
    )


def solution(mesh):
    act = P("shard", "seq", None)
    mat = P("shard", None)
    vec = P("shard")
    return jax.shard_map(
        body,
        mesh=mesh,
        in_specs=(act, act, mat, mat, mat, mat, mat, vec, mat, vec, vec, vec, vec, mat, P("shard", None, None)),
        out_specs=(act, act, mat, mat, mat, mat, mat, vec, mat, vec, vec, vec, vec),
        check_vma=False,
    )
```

```python
import jax
import jax.numpy as jnp
from jax import lax
from jax.experimental import pallas as pl
from jax.experimental.pallas import tpu as pltpu
from jax.sharding import PartitionSpec as P

H = 12
HD = 64
EPS = 1e-06
BLK=64; PAIR=128; GRP=4
F32=jnp.float32; BF=jnp.bfloat16

def nt(a,b): return lax.dot_general(a,b,(((1,),(1,)),((),())),preferred_element_type=F32)
def tn(a,b): return lax.dot_general(a,b,(((0,),(0,)),((),())),preferred_element_type=F32)
def nn(a,b): return lax.dot_general(a,b,(((1,),(0,)),((),())),preferred_element_type=F32)

def fwd_call(qkv, qmask, kmask, idx, cnt):
    seq=qkv.shape[0]; half=seq//2; nb=seq//BLK; width=qkv.shape[1]//3; pairs=width//PAIR
    rows=2*BLK; gk=GRP*BLK; maxg=nb//GRP
    def kern(idx_ref,cnt_ref,qkv_ref,qm_ref,km_ref,om_ref,os_ref,log_ref,kx,vx,s_scr,mx,acc,ls):
        lane=lax.broadcasted_iota(jnp.int32,(BLK,PAIR),1)
        low=lane<BLK
        for p in range(pairs):
            kx[p,:seq,:PAIR]=qkv_ref[:,width+p*PAIR:width+(p+1)*PAIR]
            vx[p,:seq,:]=qkv_ref[:,2*width+p*PAIR:2*width+(p+1)*PAIR]
            kx[p,seq:seq+BLK,:PAIR]=jnp.zeros((BLK,PAIR),BF)
            vx[p,seq:seq+BLK,:]=jnp.zeros((BLK,PAIR),BF)
            kx[p,:,PAIR:]=km_ref[...]
        def half_loop(out_ref,base):
            def qblock(b,_):
                i=base+b
                n=cnt_ref[i]
                qrow=pl.multiple_of(b*BLK,BLK)
                qm=qm_ref[pl.ds(pl.multiple_of(i*BLK,BLK),BLK),:]
                qs=[]
                for p in range(pairs):
                    q=qkv_ref[pl.ds(pl.multiple_of(i*BLK,BLK),BLK),p*PAIR:(p+1)*PAIR]*jnp.asarray(0.125,BF)
                    z=jnp.zeros_like(q)
                    stk=jnp.concatenate([jnp.where(low,q,z),jnp.where(low,z,q)],axis=0)
                    qs.append(jnp.concatenate([stk,jnp.concatenate([qm,qm],axis=0)],axis=1))
                    mx[p]=jnp.full((rows,PAIR),-3e38,F32)
                    ls[p]=jnp.zeros((rows,PAIR),F32)
                    acc[p]=jnp.zeros((rows,PAIR),F32)
                def p1(g,_):
                    at=[pl.multiple_of(idx_ref[i,g*GRP+j]*BLK,BLK) for j in range(GRP)]
                    for p in range(pairs):
                        kg=jnp.concatenate([kx[p,pl.ds(a,BLK),:] for a in at],axis=0)
                        s=nt(qs[p],kg)
                        s_scr[g,p]=s
                        mx[p]=jnp.maximum(mx[p],jnp.maximum(s[:,:PAIR],s[:,PAIR:]))
                    return 0
                lax.fori_loop(0,n,p1,0)
                ms=[jnp.max(mx[p],axis=1,keepdims=True) for p in range(pairs)]
                def p2(g,_):
                    at=[pl.multiple_of(idx_ref[i,g*GRP+j]*BLK,BLK) for j in range(GRP)]
                    for p in range(pairs):
                        vg=jnp.concatenate([vx[p,pl.ds(a,BLK),:] for a in at],axis=0)
                        e=jnp.exp(s_scr[g,p]-ms[p])
                        ls[p]=ls[p]+(e[:,:PAIR]+e[:,PAIR:])
                        acc[p]=acc[p]+nn(e.astype(BF),vg)
                    return 0
                lax.fori_loop(0,n,p2,0)
                lanes=lax.broadcasted_iota(jnp.int32,(rows,PAIR),1)
                logs=jnp.zeros((rows,PAIR),F32)
                for p in range(pairs):
                    l=jnp.sum(ls[p],axis=1,keepdims=True)
                    o=acc[p]*(1.0/l)
                    o=jnp.where(low,o[:BLK],o[BLK:])
                    out_ref[pl.ds(qrow,BLK),p*PAIR:(p+1)*PAIR]=o.astype(BF)
                    logs=jnp.where(lanes==p,ms[p]+jnp.log(l),logs)
                log_ref[pl.ds(pl.multiple_of(i*rows,rows),rows),:]=logs
                return 0
            lax.fori_loop(0,nb//2,qblock,0)
        half_loop(om_ref,0)
        half_loop(os_ref,nb//2)
    v=pl.BlockSpec(memory_space=pltpu.VMEM)
    s=pl.BlockSpec(memory_space=pltpu.SMEM)
    return pl.pallas_call(kern,name="attn_fwd",
        out_shape=(jax.ShapeDtypeStruct((half,width),BF),jax.ShapeDtypeStruct((half,width),BF),jax.ShapeDtypeStruct((nb*rows,PAIR),F32)),
        in_specs=[s,s,v,v,v],out_specs=(v,v,v),
        scratch_shapes=[pltpu.VMEM((pairs,seq+BLK,2*PAIR),BF),pltpu.VMEM((pairs,seq+BLK,PAIR),BF),
            pltpu.VMEM((maxg,pairs,rows,gk),F32),pltpu.VMEM((pairs,rows,PAIR),F32),pltpu.VMEM((pairs,rows,PAIR),F32),pltpu.VMEM((pairs,rows,PAIR),F32)],
        cost_estimate=pl.CostEstimate(flops=20_000_000_000,transcendentals=12_000_000,bytes_accessed=12_000_000),
    )(idx,cnt,qkv,qmask,kmask)

def bwd_call(qkv, dmine, drecv, omine, orecv, logs, qmask, kmask, idx, cnt):
    seq=qkv.shape[0]; half=seq//2; nb=seq//BLK; width=qkv.shape[1]//3; pairs=width//PAIR
    rows=2*BLK; gk=GRP*BLK
    def kern(idx_ref,cnt_ref,qkv_ref,dm_ref,dr_ref,om_ref,or_ref,log_ref,qm_ref,km_ref,g_ref,kx,vx,dk,dv,dq):
        lane=lax.broadcasted_iota(jnp.int32,(BLK,PAIR),1)
        low=lane<BLK
        for p in range(pairs):
            kx[p,:seq,:PAIR]=qkv_ref[:,width+p*PAIR:width+(p+1)*PAIR]
            vx[p,:seq,:]=qkv_ref[:,2*width+p*PAIR:2*width+(p+1)*PAIR]
            kx[p,seq:seq+BLK,:PAIR]=jnp.zeros((BLK,PAIR),BF)
            vx[p,seq:seq+BLK,:]=jnp.zeros((BLK,PAIR),BF)
            kx[p,:,PAIR:]=km_ref[...]
            dk[p]=jnp.zeros((seq+BLK,PAIR),F32)
            dv[p]=jnp.zeros((seq+BLK,PAIR),F32)
        def half_loop(o_ref,dsrc_ref,base):
            def qblock(b,_):
                i=base+b
                n=cnt_ref[i]
                qrow=pl.multiple_of(b*BLK,BLK)
                irow=pl.multiple_of(i*BLK,BLK)
                qm=qm_ref[pl.ds(irow,BLK),:]
                logs=log_ref[pl.ds(pl.multiple_of(i*rows,rows),rows),:]
                qs=[];ds_=[];ls_=[];dl=[]
                for p in range(pairs):
                    q=qkv_ref[pl.ds(pl.multiple_of(i*BLK,BLK),BLK),p*PAIR:(p+1)*PAIR]*jnp.asarray(0.125,BF)
                    z=jnp.zeros_like(q)
                    stk=jnp.concatenate([jnp.where(low,q,z),jnp.where(low,z,q)],axis=0)
                    qs.append(jnp.concatenate([stk,jnp.concatenate([qm,qm],axis=0)],axis=1))
                    d=dsrc_ref[pl.ds(qrow,BLK),p*PAIR:(p+1)*PAIR]
                    ds_.append(jnp.concatenate([jnp.where(low,d,z),jnp.where(low,z,d)],axis=0))
                    prod=d.astype(F32)*o_ref[pl.ds(qrow,BLK),p*PAIR:(p+1)*PAIR].astype(F32)
                    zf=jnp.zeros_like(prod)
                    dl.append(jnp.sum(jnp.concatenate([jnp.where(low,prod,zf),jnp.where(low,zf,prod)],axis=0),axis=1,keepdims=True))
                    ls_.append(logs[:,p:p+1])
                    dq[p]=jnp.zeros((rows,PAIR),F32)
                def step(g,_):
                    at=[pl.multiple_of(idx_ref[i,g*GRP+j]*BLK,BLK) for j in range(GRP)]
                    for p in range(pairs):
                        kg=jnp.concatenate([kx[p,pl.ds(a,BLK),:] for a in at],axis=0)
                        vg=jnp.concatenate([vx[p,pl.ds(a,BLK),:] for a in at],axis=0)
                        s=nt(qs[p],kg)
                        e=jnp.exp(s-ls_[p])
                        dp=nt(ds_[p],vg)
                        dsc=(e*(dp-dl[p])).astype(BF)
                        dq[p]=dq[p]+nn(dsc,kg[:,:PAIR])
                        dkg=tn(dsc,qs[p][:,:PAIR])
                        dvg=tn(e.astype(BF),ds_[p])
                        for j,a in enumerate(at):
                            dk[p,pl.ds(a,BLK),:]=dk[p,pl.ds(a,BLK),:]+dkg[j*BLK:(j+1)*BLK]
                            dv[p,pl.ds(a,BLK),:]=dv[p,pl.ds(a,BLK),:]+dvg[j*BLK:(j+1)*BLK]
                    return 0
                lax.fori_loop(0,n,step,0)
                for p in range(pairs):
                    g=dq[p]
                    g_ref[pl.ds(irow,BLK),p*PAIR:(p+1)*PAIR]=(jnp.where(low,g[:BLK],g[BLK:])*0.125).astype(BF)
                return 0
            lax.fori_loop(0,nb//2,qblock,0)
        half_loop(om_ref,dm_ref,0)
        half_loop(or_ref,dr_ref,nb//2)
        for p in range(pairs):
            g_ref[:,width+p*PAIR:width+(p+1)*PAIR]=dk[p,:seq].astype(BF)
            g_ref[:,2*width+p*PAIR:2*width+(p+1)*PAIR]=dv[p,:seq].astype(BF)
    v=pl.BlockSpec(memory_space=pltpu.VMEM)
    s=pl.BlockSpec(memory_space=pltpu.SMEM)
    return pl.pallas_call(kern,name="attn_bwd",
        out_shape=jax.ShapeDtypeStruct((seq,3*width),BF),
        in_specs=[s,s,v,v,v,v,v,v,v,v],out_specs=v,
        scratch_shapes=[pltpu.VMEM((pairs,seq+BLK,2*PAIR),BF),pltpu.VMEM((pairs,seq+BLK,PAIR),BF),
            pltpu.VMEM((pairs,seq+BLK,PAIR),F32),pltpu.VMEM((pairs,seq+BLK,PAIR),F32),pltpu.VMEM((pairs,rows,PAIR),F32)],
        cost_estimate=pl.CostEstimate(flops=50_000_000_000,transcendentals=12_000_000,bytes_accessed=18_000_000),
    )(idx,cnt,qkv,dmine,drecv,omine,orecv,logs,qmask,kmask)

def tables(starts, chosen, orig, seq):
    nb=orig.shape[0]
    follow=jnp.concatenate([starts[1:],jnp.full((1,),seq,jnp.int32)])-1
    fb=starts//BLK; lb=follow//BLK
    special=jnp.any(fb[None,:]==orig[:,None],axis=1)|jnp.any(lb[None,:]==orig[:,None],axis=1)
    nearby=jnp.abs(orig[:,None]-orig[None,:])<=1
    picked=jnp.any(chosen[:,:,None]==orig[None,None,:],axis=1)
    allowed=nearby|special[:,None]|special[None,:]|picked
    lo=jnp.sum((starts[None,:]<=(orig*BLK)[:,None]).astype(jnp.int32),axis=1)
    hi=jnp.sum((starts[None,:]<=(orig*BLK+BLK-1)[:,None]).astype(jnp.int32),axis=1)
    allowed=allowed&(lo[:,None]<=hi[None,:])&(lo[None,:]<=hi[:,None])
    a=allowed.astype(jnp.int32)
    before=jnp.arange(nb)
    rank=jnp.sum(jnp.where((before[None,:]<before[:,None])[None],a[:,None,:],0),axis=2)
    hit=(rank[:,:,None]==before[None,None,:])&allowed[:,:,None]
    idx=nb+jnp.sum(jnp.where(hit,before[None,:,None]-nb,0),axis=1)
    cnt=(jnp.sum(a,axis=1)+GRP-1)//GRP
    pos=(orig[:,None]*BLK+jnp.arange(BLK)[None,:]).reshape(-1)
    seg=jnp.sum((starts[None,:]<=pos[:,None]).astype(jnp.int32),axis=1)-1
    col=jnp.arange(PAIR)[None,:]
    nd=starts.shape[0]
    qmask=jnp.where((col<=nd)&(col!=seg[:,None]),-1e9,0.0).astype(BF)
    kseg=jnp.concatenate([seg,jnp.full((BLK,),nd,jnp.int32)])
    kmask=(col==kseg[:,None]).astype(BF)
    return idx.astype(jnp.int32),cnt.astype(jnp.int32),qmask,kmask


def swap(value, flip, groups):
    return lax.ppermute(value, "seq", [(s, s ^ flip) for s in range(groups)])


def cross(value, bit, shards):
    return lax.ppermute(value, "shard", [(i, i ^ (1 << bit)) for i in range(shards)])


def staged(rows, shards):
    return rows % 16 == 0 and shards & (shards - 1) == 0


def arrange(pieces, place):
    rows, width = pieces[0].shape
    count = len(pieces)

    def kern(at_ref, *refs):
        for d in range(count):
            row = pl.multiple_of((at_ref[0] ^ d) * rows, 16)
            refs[count][pl.ds(row, rows), :] = refs[d][...]

    vmem = pl.BlockSpec(memory_space=pltpu.VMEM)
    return pl.pallas_call(
        kern,
        name="arrange",
        out_shape=jax.ShapeDtypeStruct((count * rows, width), pieces[0].dtype),
        in_specs=[pl.BlockSpec(memory_space=pltpu.SMEM)] + [vmem] * count,
        out_specs=vmem,
    )(place.reshape(1), *pieces)


def gather_rows(local, place, shards):
    have = {0: local}
    for bit in reversed(range(shards.bit_length() - 1)):
        for d in list(have):
            have[d | (1 << bit)] = cross(have[d], bit, shards)
    return arrange([have[d] for d in range(shards)], place)


def sum_rows(grad, place, y, order, shards, groups):
    total, width = grad.shape
    rows = total // shards
    if not staged(rows, shards):
        share = lax.psum_scatter(grad, "shard", scatter_dimension=0, tiled=True)
        return share + swap(share, 2, groups)
    bits = shards.bit_length() - 1
    left = list(reversed(range(bits))) + ["y"]
    value = grad.reshape([2] * (bits + 1) + [rows // 2, width])
    for step in order:
        axis = left.index(step)
        mine = y if step == "y" else (place >> step) & 1
        send = lax.dynamic_index_in_dim(value, 1 - mine, axis, keepdims=False)
        keep = lax.dynamic_index_in_dim(value, mine, axis, keepdims=False)
        got = swap(send, 2, groups) if step == "y" else cross(send, step, shards)
        value = (keep.astype(F32) + got.astype(F32)).astype(BF)
        left.pop(axis)
    other = swap(value, 2, groups)
    return jnp.where(y == 0, jnp.concatenate([value, other]), jnp.concatenate([other, value]))


def join(own, other, c, width):
    a = own.reshape(own.shape[0], -1, 1, width)
    b = other.reshape(other.shape[0], -1, 1, width)
    both = jnp.where(c == 0, jnp.concatenate([a, b], 2), jnp.concatenate([b, a], 2))
    return both.reshape(own.shape[0], -1)


def take_half(full, c, width):
    parts = full.reshape(full.shape[0], -1, 2, width)
    return lax.dynamic_index_in_dim(parts, c, 2, keepdims=False).reshape(full.shape[0], -1)


def body(tokens, cotangent, query_weight, key_weight, value_weight, output_weight, inner_weight,
         inner_bias, outer_weight, first_gain, first_shift, second_gain, second_shift, doc_starts, random_blocks):
    groups = lax.axis_size("seq")
    shards = lax.axis_size("shard")
    rows, local, width = tokens.shape
    assert rows == 2 and groups == 4
    seq = local * groups
    s = lax.axis_index("seq")
    place = lax.axis_index("shard")
    c = s % 2
    y = s // 2
    hw = (H // 2) * HD
    wrows = query_weight.shape[0]
    frows = outer_weight.shape[0]
    manual = staged(wrows // 2, shards) and staged(frows // 2, shards)

    def bring(pair):
        own = lax.dynamic_index_in_dim(pair, y, 0, keepdims=False)
        return own, swap(lax.dynamic_index_in_dim(pair, 1 - y, 0, keepdims=False), 2, groups)

    def give_back(value):
        away = swap(value[local:], 2, groups)
        own = value[:local]
        return jnp.where(y == 0, jnp.stack([own, away]), jnp.stack([away, own]))

    def whole(part):
        if manual:
            return gather_rows(part, place, shards)
        return lax.all_gather(part, "shard", axis=0, tiled=True)

    x_near, x_far = bring(tokens)
    x_near_sib = swap(x_near, 1, groups)
    x_far_sib = swap(x_far, 1, groups)
    x_all = jnp.concatenate([x_near, x_far, x_near_sib, x_far_sib], axis=0)
    x = jnp.concatenate([x_near, x_far], axis=0)
    w_qkv = whole(take_half(jnp.concatenate([query_weight, key_weight, value_weight], axis=1), c, hw))
    small_local = jnp.concatenate([inner_bias, first_gain, first_shift, second_gain, second_shift])
    out_half = take_half(output_weight, c, width // 2)
    if manual:
        extra = jnp.pad(small_local, (0, 16 * (width // 2) - small_local.shape[0])).reshape(16, width // 2)
        gathered = whole(jnp.concatenate([out_half, extra], axis=0)).reshape(shards, wrows + 16, width // 2)
        out_own = gathered[:, :wrows].reshape(width, width // 2)
        small = gathered[:, wrows:].reshape(shards, -1)[:, : small_local.shape[0]]
    else:
        out_own = whole(out_half)
        small = lax.all_gather(small_local, "shard", axis=0, tiled=False)
    out_full = join(out_own, swap(out_own, 1, groups), c, width // 2)
    in_own = whole(take_half(inner_weight, c, frows // 2))
    in_sib = swap(in_own, 1, groups)
    back_own = whole(lax.dynamic_slice_in_dim(outer_weight, c * (frows // 2), frows // 2, 0))
    back_sib = swap(back_own, 1, groups)
    cot_near, cot_far = bring(cotangent)
    cot = jnp.concatenate([cot_near, cot_far], axis=0).astype(F32)
    small = small.astype(F32)
    cuts = [0]
    for item in (inner_bias, first_gain, first_shift, second_gain, second_shift):
        cuts.append(cuts[-1] + item.shape[0])
    bias, gain_one, shift_one, gain_two, shift_two = [
        small[:, a:b].reshape(-1) for a, b in zip(cuts[:-1], cuts[1:])
    ]
    bias_own = take_half(bias[None], c, frows // 2)
    bias_sib = take_half(bias[None], 1 - c, frows // 2)

    nb = seq // BLK
    per = nb // groups
    quarters = jnp.stack([s, s ^ 2, s ^ 1, s ^ 3])
    orig = (quarters[:, None] * per + jnp.arange(per)[None, :]).reshape(-1).astype(jnp.int32)
    starts = lax.dynamic_index_in_dim(doc_starts, y, 0, keepdims=False)
    chosen = lax.dynamic_index_in_dim(random_blocks, y, 0, keepdims=False)
    chosen = jnp.sum(jnp.where((orig[:, None] == jnp.arange(nb)[None, :])[:, :, None], chosen[None], 0), axis=1)
    idx, cnt, qmask, kmask = tables(starts, chosen, orig, seq)

    qkv = nn(x_all, w_qkv).astype(BF)
    ctx_own, ctx_give, logs = fwd_call(qkv, qmask, kmask, idx, cnt)
    ctx_sib = swap(ctx_give, 1, groups)
    context = join(ctx_own, ctx_sib, c, hw)
    attended = nn(context, out_full)
    res_one = x.astype(F32) + attended
    cen = res_one - jnp.mean(res_one, axis=-1, keepdims=True)
    rstd_one = lax.rsqrt(jnp.mean(cen * cen, axis=-1, keepdims=True) + EPS)
    n_one = cen * rstd_one
    first = n_one * gain_one + shift_one
    first_low = first.astype(BF)
    root = 0.7978845608028654

    def hidden(weight, bias_half):
        inner = nn(first_low, weight) + bias_half
        tanh = jnp.tanh(root * (inner + 0.044715 * inner * inner * inner))
        active = (0.5 * inner * (1.0 + tanh)).astype(BF)
        slope = 0.5 * (1.0 + tanh) + 0.5 * inner * (1.0 - tanh * tanh) * root * (1.0 + 3 * 0.044715 * inner * inner)
        return active, slope

    act_own, slope_own = hidden(in_own, bias_own)
    act_sib, slope_sib = hidden(in_sib, bias_sib)
    outer = nn(act_own, back_own) + nn(act_sib, back_sib)
    res_two = first + outer
    cen2 = res_two - jnp.mean(res_two, axis=-1, keepdims=True)
    rstd_two = lax.rsqrt(jnp.mean(cen2 * cen2, axis=-1, keepdims=True) + EPS)
    n_two = cen2 * rstd_two
    result = give_back((n_two * gain_two + shift_two).astype(BF))
    g_two = cot * gain_two
    d_second = (g_two - jnp.mean(g_two, -1, keepdims=True) - n_two * jnp.mean(g_two * n_two, -1, keepdims=True)) * rstd_two
    d_gain_two = jnp.sum(cot * n_two, axis=0)
    d_shift_two = jnp.sum(cot, axis=0)
    d_outer = d_second.astype(BF)

    def core_sum(own, give):
        return (own + swap(give.astype(BF), 1, groups).astype(F32)).astype(BF)

    top = shards.bit_length() - 1
    zs = list(range(1, top))
    back_grad = core_sum(tn(act_own, d_outer), tn(act_sib, d_outer))
    back_grad = sum_rows(back_grad, place, y, ["y", 0] + zs, shards, groups)
    di_own = (nt(d_outer, back_own) * slope_own).astype(BF)
    di_sib = (nt(d_outer, back_sib) * slope_sib).astype(BF)
    in_grad = core_sum(tn(first_low, di_own), tn(first_low, di_sib))
    in_grad = sum_rows(in_grad, place, y, [0] + zs + ["y"], shards, groups)
    d_first = d_second + nt(di_own, in_own) + nt(di_sib, in_sib)
    d_gain_one = jnp.sum(d_first * n_one, axis=0)
    d_shift_one = jnp.sum(d_first, axis=0)
    k_one = d_first * gain_one
    d_res = (k_one - jnp.mean(k_one, -1, keepdims=True) - n_one * jnp.mean(k_one * n_one, -1, keepdims=True)) * rstd_one
    d_attended = d_res.astype(BF)
    d_context = nt(d_attended, out_full).astype(BF)
    dc_own = take_half(d_context, c, hw)
    dc_recv = swap(take_half(d_context, 1 - c, hw), 1, groups)
    proj = tn(context, d_attended)
    proj = core_sum(take_half(proj, c, width // 2), take_half(proj, 1 - c, width // 2))
    proj = sum_rows(proj, place, y, ["y", 0] + zs, shards, groups)
    d_qkv = bwd_call(qkv, dc_own, dc_recv, ctx_own, ctx_give, logs, qmask, kmask, idx, cnt)
    qkv_grad = sum_rows(tn(x_all, d_qkv).astype(BF), place, y, [0] + zs + ["y"], shards, groups)
    give = nt(d_qkv[2 * local :], w_qkv).astype(BF)
    d_input = d_res + nt(d_qkv[: 2 * local], w_qkv) + swap(give, 1, groups).astype(F32)
    input_grad = give_back(d_input.astype(BF))

    db = join(jnp.sum(di_own.astype(F32), axis=0)[None], jnp.sum(di_sib.astype(F32), axis=0)[None], c, frows // 2)
    vec = [v.reshape(shards, -1) for v in (db, d_gain_one, d_shift_one, d_gain_two, d_shift_two)]
    vec = jnp.concatenate(vec, axis=1)
    for flip in (1, 2):
        vec = vec + swap(vec, flip, groups)
    for bit in range(top):
        vec = vec + cross(vec, bit, shards)
    vec = lax.dynamic_index_in_dim(vec, place, 0, keepdims=False)
    vecs = [vec[a:b] for a, b in zip(cuts[:-1], cuts[1:])]

    joined_grad = join(qkv_grad, swap(qkv_grad, 1, groups), c, hw).astype(F32)
    proj_grad = join(proj, swap(proj, 1, groups), c, width // 2).astype(F32)
    inner_grad = join(in_grad, swap(in_grad, 1, groups), c, frows // 2).astype(F32)
    back_other = swap(back_grad, 1, groups)
    outer_grad = jnp.where(
        c == 0, jnp.concatenate([back_grad, back_other]), jnp.concatenate([back_other, back_grad])
    ).astype(F32)
    return (
        result,
        input_grad,
        joined_grad[:, :width],
        joined_grad[:, width : 2 * width],
        joined_grad[:, 2 * width :],
        proj_grad,
        inner_grad,
        vecs[0],
        outer_grad,
        vecs[1],
        vecs[2],
        vecs[3],
        vecs[4],
    )


def solution(mesh):
    act = P("shard", "seq", None)
    mat = P("shard", None)
    vec = P("shard")
    return jax.shard_map(
        body,
        mesh=mesh,
        in_specs=(act, act, mat, mat, mat, mat, mat, vec, mat, vec, vec, vec, vec, mat, P("shard", None, None)),
        out_specs=(act, act, mat, mat, mat, mat, mat, vec, mat, vec, vec, vec, vec),
        check_vma=False,
    )
```
